512 devices in a mesh: mem: 64 (over z, y), lat: 8 (over x, core).
Axes of the slice: x: 4, y: 4, z: 16, core: 2. Of those that a mesh axis runs over, the one named last changes fastest.
Arguments:
- ensemble_height_winds: float32 [512, 3, 128, 1024], P('mem', None, 'lat'), may hold values from -6 to 6
- obs_count: int32 [8, 64], P('lat'), may hold values from 16 to 128, as said below
- obs_cell: int32 [8, 64, 128], P('lat'), may hold values from 0 to 255
- obs_value: float32 [8, 64, 128], P('lat'), may hold values from -6 to 6
- obs_rinv: float32 [8, 64, 128], P('lat'), may hold values from 0.5 to 8
Outputs:
- analysis: float32 [8, 64, 512, 3, 256], P('lat', 'mem')
The draws below stay inside these ranges and needn't reach their ends.
Inputs may be any that keep to these rules, and one draw needn't show every extreme that they name: `obs_count`: each region's count is 128, 64, 32 or 16, and some region has 128.
All inputs are finite; a program needn't handle non-finite values.
Results may differ from the reference program's by a relative error of at most 0.011.
Values may be sent and summed in bfloat16 or wider, within the bound.
No kernel may reach another device: no remote copies, remote signals or barrier semaphores. Data moves between devices by JAX's collectives and lax.ppermute only.
A program may use at most 64 MiB of HBM per device.

```python
import math
import jax
import jax.numpy as jnp
from jax import lax

ENSEMBLE_SIZE = 512
PATCH_EDGE_LEN = 16
PMAX = 128
NS_ITERS = 5
PATCH_POINTS = 256
NLAT = 128
NLON = 1024
PATCH_DOWN = 8
PATCH_ACROSS = 64


def draw_obs_count(key, part):
    level_key = jax.random.fold_in(key, 11)
    spot_key = jax.random.fold_in(key, 23)
    level_ids = jax.random.randint(level_key, (PATCH_DOWN * PATCH_ACROSS,), 0, 4)
    divisor = jnp.take(jnp.array([1, 2, 4, 8], dtype=jnp.int32), level_ids)
    counts = PMAX // divisor
    chosen = jax.random.randint(spot_key, (), 0, PATCH_DOWN * PATCH_ACROSS)
    counts = jnp.where(jnp.arange(PATCH_DOWN * PATCH_ACROSS) == chosen, PMAX, counts)
    return counts.reshape(PATCH_DOWN, PATCH_ACROSS).astype(jnp.int32)


def place_ends(values, own_key, smallest, largest):
    place = [jax.random.randint(jax.random.fold_in(own_key, axis), (), 0, length) for axis, length in enumerate(values.shape)]
    widest = values.shape.index(max(values.shape))
    next_to = place[:widest] + [(place[widest] + 1) % values.shape[widest]] + place[widest + 1:]
    return values.at[tuple(place)].set(smallest).at[tuple(next_to)].set(largest)


def block_levels(stream_key, extent, cuts, least, largest):
    factor_of = 1.0
    for axis_at, parts in cuts:
        steps = jax.random.uniform(jax.random.fold_in(jax.random.fold_in(stream_key, 6), axis_at), (parts,), jnp.float32, least / len(cuts), largest / len(cuts))
        factor_of = factor_of * jnp.repeat(jnp.exp(steps), extent[axis_at] // parts).reshape((-1,) + (1,) * (len(extent) - 1 - axis_at))
    return factor_of


def scatter_about(stream_key, shape, width, bound, shards=(), kind=jnp.bfloat16):
    values = jax.random.normal(stream_key, shape, jnp.float32) * width
    if len(shards) > 0:
        values = block_levels(stream_key, shape, shards, -0.22, 0.18) * values
    return jnp.clip(values, min=-bound, max=bound).astype(kind)


def setup_inputs(seed: int = 0) -> dict:
    keys = jax.random.split(jax.random.key(seed), 6)
    return {
        "ensemble_height_winds": scatter_about(keys[0], (ENSEMBLE_SIZE, 3, NLAT, NLON), 0.5, 6.0, ((0, 64), (2, 8)), jnp.float32),
        "obs_count": draw_obs_count(jax.random.fold_in(keys[5], 71), 0),
        "obs_cell": place_ends(jax.random.randint(keys[2], (PATCH_DOWN, PATCH_ACROSS, PMAX), 0, PATCH_POINTS), jax.random.fold_in(keys[2], 1), 0, PATCH_POINTS - 1).astype(jnp.int32),
        "obs_value": scatter_about(keys[3], (PATCH_DOWN, PATCH_ACROSS, PMAX), 1.0, 6.0, ((0, 8),), jnp.float32),
        "obs_rinv": jnp.clip(jnp.exp(math.log(8.0) - 2.7725887 * jax.random.uniform(keys[4], (PATCH_DOWN, PATCH_ACROSS, PMAX), jnp.float32) ** block_levels(keys[4], (PATCH_DOWN, PATCH_ACROSS, PMAX), ((0, 8),), -0.2, 0.2)), 0.5, 8.0),
    }


GRAVITY = 1.0
DEPTH = 1.0
CORIOLIS = 0.25
TIME_STEP = 0.5
EDGE_WEIGHT = 0.6
CORNER_WEIGHT = 0.35
NEWTON_SCALE = 16.0

def tendency(padded):
    height = padded[..., 0, :, :]
    east_wind = padded[..., 1, :, :]
    north_wind = padded[..., 2, :, :]

    def along_x(quantity):
        return (quantity[..., 1:-1, 2:] - quantity[..., 1:-1, :-2]) * 0.5

    def along_y(quantity):
        return (quantity[..., 2:, 1:-1] - quantity[..., :-2, 1:-1]) * 0.5
    east_mid = east_wind[..., 1:-1, 1:-1]
    north_mid = north_wind[..., 1:-1, 1:-1]
    flux_x = (DEPTH + height) * east_wind
    flux_y = (DEPTH + height) * north_wind
    rate_height = -(along_x(flux_x) + along_y(flux_y))
    rate_east = -(east_mid * along_x(east_wind) + north_mid * along_y(east_wind)) + CORIOLIS * north_mid - GRAVITY * along_x(height)
    rate_north = -(east_mid * along_x(north_wind) + north_mid * along_y(north_wind)) - CORIOLIS * east_mid - GRAVITY * along_y(height)
    return jnp.stack([rate_height, rate_east, rate_north], axis=-3)

def explicit_integrator(gridded_numbers):

    def with_zeros(quantity):
        return jnp.pad(quantity, ((0, 0), (1, 1), (1, 1)))
    section_one = gridded_numbers + TIME_STEP * tendency(with_zeros(gridded_numbers))
    section_two = 0.75 * gridded_numbers + 0.25 * (section_one + TIME_STEP * tendency(with_zeros(section_one)))
    return gridded_numbers / 3.0 + 2.0 / 3.0 * (section_two + TIME_STEP * tendency(with_zeros(section_two)))

def make_block(equivalents, number, measured, precision):
    ensemble = equivalents.shape[0]
    centre = lax.optimization_barrier(jnp.mean(equivalents, axis=0))
    slot_ids = jnp.arange(equivalents.shape[1], dtype=jnp.int32)
    weight = jnp.where(slot_ids < number, jnp.sqrt(precision), 0.0)
    scaled = (weight[:, None] * (equivalents.T - centre[:, None]) / math.sqrt(ensemble - 1)).astype(jnp.bfloat16)
    misfit = weight * (measured - centre)
    summary = jnp.dot(misfit, scaled.astype(jnp.float32), precision=lax.Precision.HIGHEST)
    return jnp.concatenate([scaled, summary.astype(jnp.bfloat16)[None, :]], axis=0)

def centre_region(region):
    flat_state = region.reshape(region.shape[0], -1)
    ens_mean = lax.optimization_barrier(jnp.mean(flat_state, axis=0))
    return (ens_mean, (flat_state - ens_mean).astype(jnp.bfloat16))

def analyse(neighbourhood, ens_mean, deviations):
    ensemble = deviations.shape[0]
    obs_slots = neighbourhood.shape[2] - 1
    locality = [[CORNER_WEIGHT, EDGE_WEIGHT, CORNER_WEIGHT], [EDGE_WEIGHT, 1.0, EDGE_WEIGHT], [CORNER_WEIGHT, EDGE_WEIGHT, CORNER_WEIGHT]]
    gram_sum = jnp.zeros((ensemble, ensemble), jnp.float32)
    mean_drive = jnp.zeros((ensemble,), jnp.float32)
    for row_off in range(3):
        for col_off in range(3):
            factor = locality[row_off][col_off]
            scaled = neighbourhood[row_off, col_off, :obs_slots]
            gram_sum = gram_sum + factor * lax.dot_general(scaled, scaled, (((0,), (0,)), ((), ())), preferred_element_type=jnp.float32)
            mean_drive = mean_drive + factor * neighbourhood[row_off, col_off, obs_slots].astype(jnp.float32)
    identity = jnp.eye(ensemble, dtype=jnp.float32)
    root_half = ((identity + gram_sum) / NEWTON_SCALE).astype(jnp.bfloat16)
    root_inverse = identity.astype(jnp.bfloat16)
    for sweep in range(NS_ITERS):
        product = jnp.dot(root_inverse, root_half, preferred_element_type=jnp.float32)
        correction = (1.5 * identity - 0.5 * product).astype(jnp.bfloat16)
        root_half = jnp.dot(root_half, correction, preferred_element_type=jnp.float32).astype(jnp.bfloat16)
        root_inverse = jnp.dot(correction, root_inverse, preferred_element_type=jnp.float32).astype(jnp.bfloat16)
    inverse_full = root_inverse.astype(jnp.float32)
    inner_step = jnp.dot(inverse_full, mean_drive, precision=lax.Precision.HIGHEST)
    mean_weights = jnp.dot(inverse_full, inner_step, precision=lax.Precision.HIGHEST) / NEWTON_SCALE
    transform = (mean_weights[:, None] / math.sqrt(ensemble - 1) + inverse_full / math.sqrt(NEWTON_SCALE)).astype(jnp.bfloat16)
    return ens_mean + lax.dot_general(transform, deviations, (((0,), (0,)), ((), ())), preferred_element_type=jnp.float32)

def reference(ensemble_height_winds, obs_count, obs_cell, obs_value, obs_rinv):
    propagate_ahead = lax.map(explicit_integrator, ensemble_height_winds)
    patch_sequence = propagate_ahead.reshape(ENSEMBLE_SIZE, 3, PATCH_DOWN, PATCH_EDGE_LEN, PATCH_ACROSS, PATCH_EDGE_LEN).transpose(2, 4, 0, 1, 3, 5).reshape(PATCH_DOWN * PATCH_ACROSS, ENSEMBLE_SIZE, 3, PATCH_POINTS)
    means, devs = lax.map(centre_region, patch_sequence)

    def one_block(inputs):
        deviation, cell_ids, number, measured, precision = inputs
        heights = deviation[:, :PATCH_POINTS].astype(jnp.float32)
        return make_block(jnp.take(heights, cell_ids, axis=1), number, measured, precision)
    blocks = lax.map(one_block, (devs, obs_cell.reshape(PATCH_DOWN * PATCH_ACROSS, PMAX), obs_count.reshape(PATCH_DOWN * PATCH_ACROSS), obs_value.reshape(PATCH_DOWN * PATCH_ACROSS, PMAX), obs_rinv.reshape(PATCH_DOWN * PATCH_ACROSS, PMAX)))
    blocks = blocks.reshape(PATCH_DOWN, PATCH_ACROSS, PMAX + 1, ENSEMBLE_SIZE)
    padded_blocks = jnp.pad(blocks, ((1, 1), (1, 1), (0, 0), (0, 0)))
    zero_index = jnp.zeros((), jnp.int32)

    def one_region(region_index):
        row_at = (region_index // PATCH_ACROSS).astype(jnp.int32)
        col_at = (region_index % PATCH_ACROSS).astype(jnp.int32)
        neighbourhood = lax.dynamic_slice(padded_blocks, (row_at, col_at, zero_index, zero_index), (3, 3, PMAX + 1, ENSEMBLE_SIZE))
        ens_mean = lax.dynamic_index_in_dim(means, region_index, 0, keepdims=False)
        deviation = lax.dynamic_index_in_dim(devs, region_index, 0, keepdims=False)
        return analyse(neighbourhood, ens_mean, deviation)
    result = lax.map(one_region, jnp.arange(PATCH_DOWN * PATCH_ACROSS, dtype=jnp.int32))
    return result.reshape(PATCH_DOWN, PATCH_ACROSS, ENSEMBLE_SIZE, 3, PATCH_POINTS)
```

```python
import math


import jax
import jax.numpy as jnp
from jax import lax
from jax.experimental import pallas as pl
from jax.experimental.pallas import tpu as pltpu
from jax.sharding import PartitionSpec as P

EDGE = 16
NS_ITERS = 5
EDGE_WEIGHT = 0.6
CORNER_WEIGHT = 0.35
NEWTON_SCALE = 16.0
HALO = 3
LANES = 128

bf16 = jnp.bfloat16
f32 = jnp.float32


def vmem_spec():
    return pl.BlockSpec(memory_space=pltpu.VMEM)


def smem_spec():
    return pl.BlockSpec(memory_space=pltpu.SMEM)


def tile_shifts(load, n, lane):
    tiles, ahead, behind = {}, {}, {}

    def get(t):
        if t not in tiles:
            tiles[t] = load(t)
            ahead[t] = pltpu.roll(tiles[t], LANES - 1, 1)
            behind[t] = pltpu.roll(tiles[t], 1, 1)

    def at(t):
        get(t)
        if t + 1 < n:
            get(t + 1)
        edge = ahead[t + 1] if t + 1 < n else jnp.zeros_like(tiles[t])
        plus = jnp.where(lane == LANES - 1, edge, ahead[t])
        edge = behind[t - 1] if t > 0 else jnp.zeros_like(tiles[t])
        minus = jnp.where(lane == 0, edge, behind[t])
        return tiles[t], plus - minus

    return at


def advance(src, i, lane, n_tiles):
    def load(f, k):
        return lambda t: src[f, k, :, t * LANES : (t + 1) * LANES]

    h_at = tile_shifts(load(0, i), n_tiles, lane)
    u_at = tile_shifts(load(1, i), n_tiles, lane)
    v_at = tile_shifts(load(2, i), n_tiles, lane)
    flux_at = tile_shifts(
        lambda t: (1.0 + load(0, i)(t)) * load(1, i)(t), n_tiles, lane
    )
    for t in range(n_tiles):
        h, dh = h_at(t)
        u, du = u_at(t)
        v, dv = v_at(t)
        _, df = flux_at(t)
        hu, hd = load(0, i + 1)(t), load(0, i - 1)(t)
        vu, vd = load(2, i + 1)(t), load(2, i - 1)(t)
        dyu = load(1, i + 1)(t) - load(1, i - 1)(t)
        dyf = (1.0 + hu) * vu - (1.0 + hd) * vd
        qu, qv = 0.25 * u, 0.25 * v
        yield t, (
            h - 0.25 * (df + dyf),
            u - (qu * du + qv * (dyu - 0.5) + 0.25 * dh),
            v - (qu * (dv + 0.5) + qv * (vu - vd) + 0.25 * (hu - hd)),
        )


def edge_kernel(x_ref, first_ref, last_ref, sems):
    rows = x_ref.shape[2]
    copies = []
    for f in range(3):
        for k in range(HALO):
            for e, (dst, r) in enumerate(((first_ref, k), (last_ref, rows - HALO + k))):
                copies.append(
                    pltpu.make_async_copy(x_ref.at[:, f, r], dst.at[f, k], sems.at[(f * HALO + k) * 2 + e])
                )
    for c in copies:
        c.start()
    for c in copies:
        c.wait()


def edge_rows(x):
    members, fields, _, columns = x.shape
    part = jax.ShapeDtypeStruct((fields, HALO, members, columns), f32)
    return pl.pallas_call(
        edge_kernel,
        out_shape=(part, part),
        in_specs=[pl.BlockSpec(memory_space=pl.ANY)],
        out_specs=(vmem_spec(), vmem_spec()),
        scratch_shapes=[pltpu.SemaphoreType.DMA((fields * HALO * 2,))],
        compiler_params=pltpu.CompilerParams(vmem_limit_bytes=4 << 20),
        name="edges",
    )(x)


def inner_kernel(x_ref, s3_ref, s1e_ref, s2e_ref, q, a, b, sems):
    rows = x_ref.shape[2]
    n_tiles = x_ref.shape[3] // LANES
    copies = [
        pltpu.make_async_copy(x_ref.at[:, f, r], q.at[f, r], sems.at[f * rows + r])
        for r in range(rows)
        for f in range(3)
    ]
    for c in copies:
        c.start()
    for c in copies:
        c.wait()
    lane = lax.broadcasted_iota(jnp.int32, (8, LANES), 1)

    def section(src, dst, lo, hi, off, combine):
        @pl.loop(lo, hi, unroll=2)
        def _(i):
            for t, new in advance(src, i, lane, n_tiles):
                sl = slice(t * LANES, (t + 1) * LANES)
                for f in range(3):
                    dst[f, i - off, :, sl] = combine(new[f], lambda: q[f, i, :, sl])

    section(q, a, 1, rows - 1, 0, lambda s, q0: s)
    section(a, b, 2, rows - 2, 0, lambda s, q0: 0.75 * q0() + 0.25 * s)
    section(b, s3_ref, 3, rows - 3, 3, lambda s, q0: q0() * (1.0 / 3.0) + (2.0 / 3.0) * s)
    s1e_ref[:, :2] = a[:, 1:3]
    s1e_ref[:, 2:] = a[:, rows - 3 : rows - 1]
    s2e_ref[:, :2] = b[:, 2:4]
    s2e_ref[:, 2:] = b[:, rows - 4 : rows - 2]


def inner_forecast(x):
    members, fields, rows, columns = x.shape

    def part(n):
        return jax.ShapeDtypeStruct((fields, n, members, columns), f32)

    return pl.pallas_call(
        inner_kernel,
        out_shape=(part(rows - 2 * HALO), part(4), part(4)),
        in_specs=[pl.BlockSpec(memory_space=pl.ANY)],
        out_specs=(vmem_spec(),) * 3,
        scratch_shapes=[pltpu.VMEM((fields, rows, members, columns), f32)] * 3
        + [pltpu.SemaphoreType.DMA((fields * rows,))],
        compiler_params=pltpu.CompilerParams(vmem_limit_bytes=12 << 20),
        cost_estimate=pl.CostEstimate(flops=4 * 10**8, bytes_accessed=4 * 10**6, transcendentals=0),
        name="inner",
    )(x)


def outer_kernel(
    row_ref, top_ref, first_ref, last_ref, bottom_ref, s1e_ref, s2e_ref, s3_ref, h_ref, uv_ref, q, a, b, c
):
    rows = s3_ref.shape[1] + 2 * HALO
    n_tiles = s3_ref.shape[3] // LANES
    lane = lax.broadcasted_iota(jnp.int32, (8, LANES), 1)
    q[:, 0:3] = top_ref[...]
    q[:, 3:6] = first_ref[...]
    q[:, 6:9] = last_ref[...]
    q[:, 9:12] = bottom_ref[...]
    a[:, 3:7] = s1e_ref[...]
    b[:, 3:7] = s2e_ref[...]

    def section(src, dst, centre_jump, dst_jump, q_at, combine):
        @pl.loop(0, 2 * HALO, unroll=6)
        def _(i):
            low = (i >= HALO).astype(jnp.int32)
            at, to, qi = i + 1 + centre_jump * low, i + dst_jump * low, q_at(i, low)
            for t, new in advance(src, at, lane, n_tiles):
                sl = slice(t * LANES, (t + 1) * LANES)
                for f in range(3):
                    dst[f, to, :, sl] = combine(new[f], lambda: q[f, qi, :, sl])

    def clear(ref, top_at, bottom_at):
        @pl.when(row_ref[0] == 0)
        def _():
            ref[:, top_at] = jnp.zeros_like(ref[:, top_at])

        @pl.when(row_ref[0] == row_ref[1] - 1)
        def _():
            ref[:, bottom_at] = jnp.zeros_like(ref[:, bottom_at])

    section(q, a, 4, 4, lambda i, low: i, lambda s, q0: s)
    clear(a, 1, 8)
    section(a, b, 2, 4, lambda i, low: i + 2 + 2 * low, lambda s, q0: 0.75 * q0() + 0.25 * s)
    clear(b, 0, 9)
    section(b, c, 2, 0, lambda i, low: i + 3, lambda s, q0: q0() * (1.0 / 3.0) + (2.0 / 3.0) * s)

    block = lane // EDGE
    keep = {bit: (block & bit) == 0 for bit in (1, 2, 4)}

    def final_row(f, r, col):
        if r < HALO:
            return c[f, r, :, col]
        if r >= rows - HALO:
            return c[f, r - rows + 2 * HALO, :, col]
        return s3_ref[f, r - HALO, :, col]

    @pl.loop(0, n_tiles)
    def _(t):
        col = pl.ds(pl.multiple_of(t * LANES, LANES), LANES)
        for f in range(3):
            for half in range(rows // 8):
                v = [final_row(f, half * 8 + r, col) for r in range(8)]
                for bit in (4, 2, 1):
                    for i in range(8):
                        if i & bit:
                            continue
                        lo, hi = v[i], v[i | bit]
                        v[i] = jnp.where(keep[bit], lo, pltpu.roll(hi, bit * EDGE, 1))
                        v[i | bit] = jnp.where(keep[bit], pltpu.roll(lo, LANES - bit * EDGE, 1), hi)
                for d in range(8):
                    if f == 0:
                        h_ref[t * 8 + d, half] = v[d].astype(bf16)
                    else:
                        uv_ref[t * 8 + d, (f - 1) * 2 + half] = v[d].astype(bf16)


def outer_forecast(row, top, first, last, bottom, s1e, s2e, s3):
    fields, _, members, columns = s3.shape
    n_dest = columns // EDGE

    def scratch(n):
        return pltpu.VMEM((fields, n, members, columns), f32)

    return pl.pallas_call(
        outer_kernel,
        out_shape=(
            jax.ShapeDtypeStruct((n_dest, 2, members, LANES), bf16),
            jax.ShapeDtypeStruct((n_dest, 4, members, LANES), bf16),
        ),
        in_specs=[smem_spec()] + [vmem_spec()] * 7,
        out_specs=(vmem_spec(), vmem_spec()),
        scratch_shapes=[scratch(12), scratch(10), scratch(10), scratch(6)],
        compiler_params=pltpu.CompilerParams(vmem_limit_bytes=16 << 20),
        cost_estimate=pl.CostEstimate(flops=2 * 10**8, bytes_accessed=4 * 10**6, transcendentals=0),
        name="outer",
    )(row, top, first, last, bottom, s1e, s2e, s3)


def split3(row):
    high = row.astype(bf16)
    rest = row - high.astype(f32)
    mid = rest.astype(bf16)
    low = (rest - mid.astype(f32)).astype(bf16)
    zero = jnp.zeros((5, row.shape[1]), f32)
    return jnp.concatenate([high.astype(f32), mid.astype(f32), low.astype(f32), zero], axis=0).astype(bf16)


def centred(slab):
    value = slab.astype(f32).reshape(-1, LANES)
    mean = jnp.sum(value, axis=0, keepdims=True) * (1.0 / value.shape[0])
    return mean, (value - mean).astype(bf16)


def block_kernel(at_ref, count_ref, cell_ref, value_ref, rinv_ref, h_ref, out_ref):
    at = at_ref[0]
    members = h_ref.shape[0] * h_ref.shape[2]
    slots = cell_ref.shape[1]
    cell = cell_ref[pl.ds(at, 1), :]
    value = value_ref[pl.ds(at, 1), :]
    rinv = rinv_ref[pl.ds(at, 1), :]
    hx = jnp.zeros((members, slots), f32)
    for half in range(2):
        _, deviation = centred(h_ref[:, half])
        place = lax.broadcasted_iota(jnp.int32, (LANES, slots), 0) + half * LANES
        pick = jnp.where(place == cell, 1.0, 0.0).astype(bf16)
        hx = hx + jnp.dot(deviation, pick, preferred_element_type=f32)
    centre = jnp.sum(hx, axis=0, keepdims=True) * (1.0 / members)
    slot = lax.broadcasted_iota(jnp.int32, (1, slots), 1)
    weight = jnp.where(slot < count_ref[0, at], jnp.sqrt(rinv), 0.0)
    scaled = (weight * (hx - centre) * (1.0 / math.sqrt(members - 1))).astype(bf16)
    misfit = weight * (value - centre)
    summary = lax.dot_general(
        split3(misfit), scaled, (((1,), (1,)), ((), ())), preferred_element_type=f32
    )
    summary = jnp.sum(summary, axis=0, keepdims=True)
    out_ref[:members] = scaled
    pieces = [summary[:, i * LANES : (i + 1) * LANES] for i in range(members // LANES)]
    pieces.append(jnp.zeros((8 - len(pieces), LANES), f32))
    out_ref[members:] = jnp.concatenate(pieces, axis=0).astype(bf16)


def make_block(at, count, cell, value, rinv, h):
    members = h.shape[0] * h.shape[2]
    return pl.pallas_call(
        block_kernel,
        out_shape=jax.ShapeDtypeStruct((members + 8, cell.shape[1]), bf16),
        in_specs=[smem_spec(), smem_spec()] + [vmem_spec()] * 4,
        out_specs=vmem_spec(),
        name="block",
        compiler_params=pltpu.CompilerParams(vmem_limit_bytes=16 << 20),
    )(at, count, cell, value, rinv, h)


def transform_kernel(own_ref, west_ref, east_ref, north_ref, south_ref, out_ref):
    n = out_ref.shape[0]

    def gram_of(refs):
        y = jnp.concatenate([r[:n] for r in refs], axis=1)
        return lax.dot_general(y, y, (((1,), (1,)), ((), ())), preferred_element_type=f32)

    def drive_of(refs):
        total = refs[0][n:].astype(f32)
        for r in refs[1:]:
            total = total + r[n:].astype(f32)
        return total

    centre = [own_ref]
    edges = [west_ref, east_ref, north_ref.at[1], south_ref.at[1]]
    corners = [north_ref.at[0], north_ref.at[2], south_ref.at[0], south_ref.at[2]]
    drive = drive_of(centre) + EDGE_WEIGHT * drive_of(edges) + CORNER_WEIGHT * drive_of(corners)
    drive = jnp.concatenate([drive[i : i + 1] for i in range(n // LANES)], axis=1)
    gram = gram_of(centre) + EDGE_WEIGHT * gram_of(edges) + CORNER_WEIGHT * gram_of(corners)
    diagonal = lax.broadcasted_iota(jnp.int32, (n, n), 0) == lax.broadcasted_iota(jnp.int32, (n, n), 1)
    half_scale = 1.0 / NEWTON_SCALE
    root = (gram * half_scale + jnp.where(diagonal, half_scale, 0.0)).astype(bf16)
    shifted = jnp.where(diagonal, 1.5, 0.0)
    product = root.astype(f32)
    inverse = None
    for sweep in range(NS_ITERS):
        if sweep > 0:
            product = jnp.dot(root, inverse, preferred_element_type=f32)
        correction = (shifted - 0.5 * product).astype(bf16)
        if sweep + 1 < NS_ITERS:
            root = jnp.dot(correction, root, preferred_element_type=f32).astype(bf16)
        if sweep == 0:
            inverse = correction
        else:
            inverse = jnp.dot(inverse, correction, preferred_element_type=f32).astype(bf16)

    def apply(row):
        return jnp.sum(jnp.dot(split3(row), inverse, preferred_element_type=f32), axis=0, keepdims=True)

    weights = apply(apply(drive)) * (1.0 / NEWTON_SCALE / math.sqrt(n - 1))
    out_ref[...] = (weights + inverse.astype(f32) * (1.0 / math.sqrt(NEWTON_SCALE))).astype(bf16)


def make_transform(own, west, east, north, south):
    n = own.shape[0] - 8
    return pl.pallas_call(
        transform_kernel,
        out_shape=jax.ShapeDtypeStruct((n, n), bf16),
        in_specs=[vmem_spec()] * 5,
        out_specs=vmem_spec(),
        name="transform",
        compiler_params=pltpu.CompilerParams(vmem_limit_bytes=24 << 20),
    )(own, west, east, north, south)


def analysis_kernel(transform_ref, h_ref, uv_ref, out_ref):
    for f in range(3):
        src = h_ref if f == 0 else uv_ref
        for half in range(2):
            mean, deviation = centred(src[:, half + 2 * max(f - 1, 0)])
            out_ref[f, :, half * LANES : (half + 1) * LANES] = mean + jnp.dot(
                transform_ref[...], deviation, preferred_element_type=f32
            )


def analyse(transform, h, uv):
    n = transform.shape[0]
    return pl.pallas_call(
        analysis_kernel,
        out_shape=jax.ShapeDtypeStruct((3, n, EDGE * EDGE), f32),
        in_specs=[vmem_spec()] * 3,
        out_specs=vmem_spec(),
        name="analysis",
        compiler_params=pltpu.CompilerParams(vmem_limit_bytes=16 << 20),
    )(transform, h, uv)


def both_ways(before_part, after_part, axis):
    size = lax.axis_size(axis)
    up = [(i, i + 1) for i in range(size - 1)]
    down = [(j, i) for i, j in up]
    return lax.ppermute(after_part, axis, up), lax.ppermute(before_part, axis, down)


def per_device(ensemble_height_winds, obs_count, obs_cell, obs_value, obs_rinv):
    x = ensemble_height_winds
    at = lax.axis_index("mem").astype(jnp.int32).reshape(1)
    row = jnp.stack([lax.axis_index("lat"), lax.axis_size("lat")]).astype(jnp.int32)

    first, last = edge_rows(x)
    top, bottom = both_ways(first, last, "lat")
    s3, s1e, s2e = inner_forecast(x)
    h, uv = outer_forecast(row, top, first, last, bottom, s1e, s2e, s3)

    def exchange(part):
        return lax.all_to_all(part, "mem", split_axis=0, concat_axis=0, tiled=True)

    h = exchange(h)
    own = make_block(at, obs_count, obs_cell[0], obs_value[0], obs_rinv[0], h)
    uv, own = lax.optimization_barrier((uv, own))
    uv = exchange(uv)
    west, east = both_ways(own, own, "mem")
    line = jnp.stack([west, own, east])
    north, south = both_ways(line, line, "lat")
    transform = make_transform(own, west, east, north, south)
    analysed = analyse(transform, h, uv)
    return analysed.transpose(1, 0, 2)[None, None]


def solution(mesh):
    in_specs = (
        P("mem", None, "lat", None),
        P("lat", None),
        P("lat", None, None),
        P("lat", None, None),
        P("lat", None, None),
    )
    out_specs = P("lat", "mem", None, None, None)
    return jax.shard_map(
        per_device, mesh=mesh, in_specs=in_specs, out_specs=out_specs, check_vma=False
    )
```

```python
import functools
import math


import jax
import jax.numpy as jnp
from jax import lax
from jax.experimental import pallas as pl
from jax.experimental.pallas import tpu as pltpu
from jax.sharding import PartitionSpec as P

EDGE = 16
NS_ITERS = 5
EDGE_WEIGHT = 0.6
CORNER_WEIGHT = 0.35
NEWTON_SCALE = 16.0
HALO = 3
RING = 4
LANES = 128

bf16 = jnp.bfloat16
f32 = jnp.float32


def vmem_spec():
    return pl.BlockSpec(memory_space=pltpu.VMEM)


def smem_spec():
    return pl.BlockSpec(memory_space=pltpu.SMEM)


def tile_shifts(load, n, lane):
    tiles, ahead, behind = {}, {}, {}

    def get(t):
        if t not in tiles:
            tiles[t] = load(t)
            ahead[t] = pltpu.roll(tiles[t], LANES - 1, 1)
            behind[t] = pltpu.roll(tiles[t], 1, 1)

    def at(t):
        get(t)
        if t + 1 < n:
            get(t + 1)
        edge = ahead[t + 1] if t + 1 < n else jnp.zeros_like(tiles[t])
        plus = jnp.where(lane == LANES - 1, edge, ahead[t])
        edge = behind[t - 1] if t > 0 else jnp.zeros_like(tiles[t])
        minus = jnp.where(lane == 0, edge, behind[t])
        return tiles[t], plus - minus

    return at


def advance(src, i, lane, n_tiles, fields=(0, 1, 2)):
    def load(f, k):
        return lambda t: src[f, k, :, t * LANES : (t + 1) * LANES]

    h_at = tile_shifts(load(0, i), n_tiles, lane)
    u_at = tile_shifts(load(1, i), n_tiles, lane)
    v_at = tile_shifts(load(2, i), n_tiles, lane)
    flux_at = tile_shifts(
        lambda t: (1.0 + load(0, i)(t)) * load(1, i)(t), n_tiles, lane
    )
    for t in range(n_tiles):
        hu, hd = load(0, i + 1)(t), load(0, i - 1)(t)
        vu, vd = load(2, i + 1)(t), load(2, i - 1)(t)
        new = []
        if 0 in fields:
            _, df = flux_at(t)
            dyf = (1.0 + hu) * vu - (1.0 + hd) * vd
            new.append(load(0, i)(t) - 0.25 * (df + dyf))
        if 1 in fields:
            _, dh = h_at(t)
            u, du = u_at(t)
            v, dv = v_at(t)
            dyu = load(1, i + 1)(t) - load(1, i - 1)(t)
            qu, qv = 0.25 * u, 0.25 * v
            new.append(u - (qu * du + qv * (dyu - 0.5) + 0.25 * dh))
            new.append(v - (qu * (dv + 0.5) + qv * (vu - vd) + 0.25 * (hu - hd)))
        yield t, new


def edge_kernel(row_ref, q_ref, near_ref, far_ref):
    rows = q_ref.shape[1]

    def place(first_ref, last_ref):
        first_ref[...] = q_ref[:, :HALO]
        last_ref[...] = q_ref[:, rows - HALO :]

    @pl.when(row_ref[0] % 2 == 0)
    def _():
        place(far_ref, near_ref)

    @pl.when(row_ref[0] % 2 == 1)
    def _():
        place(near_ref, far_ref)


def edge_rows(row, q):
    fields, _, members, columns = q.shape
    part = jax.ShapeDtypeStruct((fields, HALO, members, columns), f32)
    return pl.pallas_call(
        edge_kernel,
        out_shape=(part, part),
        in_specs=[smem_spec(), vmem_spec()],
        out_specs=(vmem_spec(), vmem_spec()),
        compiler_params=pltpu.CompilerParams(vmem_limit_bytes=4 << 20),
        name="edges",
    )(row, q)


def inner_kernel(q, s3_ref, s1e_ref, s2e_ref, a, b):
    rows = q.shape[1]
    n_tiles = q.shape[3] // LANES
    lane = lax.broadcasted_iota(jnp.int32, (8, LANES), 1)

    def section(src, dst, lo, hi, off, combine):
        @pl.loop(lo, hi, unroll=2)
        def _(i):
            for t, new in advance(src, i, lane, n_tiles):
                sl = slice(t * LANES, (t + 1) * LANES)
                for f in range(3):
                    dst[f, i - off, :, sl] = combine(new[f], lambda: q[f, i, :, sl])

    section(q, a, 1, rows - 1, 0, lambda s, q0: s)
    section(a, b, 2, rows - 2, 0, lambda s, q0: 0.75 * q0() + 0.25 * s)
    section(b, s3_ref, 3, rows - 3, 3, lambda s, q0: q0() * (1.0 / 3.0) + (2.0 / 3.0) * s)
    s1e_ref[:, :2] = a[:, 1:3]
    s1e_ref[:, 2:] = a[:, rows - 3 : rows - 1]
    s2e_ref[:, :2] = b[:, 2:4]
    s2e_ref[:, 2:] = b[:, rows - 4 : rows - 2]


def inner_forecast(q):
    fields, rows, members, columns = q.shape

    def part(n):
        return jax.ShapeDtypeStruct((fields, n, members, columns), f32)

    return pl.pallas_call(
        inner_kernel,
        out_shape=(part(rows - 2 * HALO), part(4), part(4)),
        in_specs=[vmem_spec()],
        out_specs=(vmem_spec(),) * 3,
        scratch_shapes=[pltpu.VMEM((fields, rows, members, columns), f32)] * 2,
        compiler_params=pltpu.CompilerParams(vmem_limit_bytes=12 << 20),
        cost_estimate=pl.CostEstimate(flops=4 * 10**8, bytes_accessed=4 * 10**6, transcendentals=0),
        name="inner",
    )(q)


def edge_section(src, dst, lane, n_tiles, fields, places, combine):
    @pl.loop(0, 2 * HALO, unroll=2 * HALO)
    def _(i):
        at, to, q_row = places(i, (i >= HALO).astype(jnp.int32))
        for t, new in advance(src, at, lane, n_tiles, fields):
            sl = slice(t * LANES, (t + 1) * LANES)
            for k, f in enumerate(fields):
                dst[f - fields[0], to, :, sl] = combine(new[k], lambda: q_row(f, sl))


def final_section(lane, n_tiles, fields, q_row, b, c):
    for i in range(2 * HALO):
        at = i + 1 if i < HALO else i + 3
        for t, new in advance(b, at, lane, n_tiles, fields):
            sl = slice(t * LANES, (t + 1) * LANES)
            for k, f in enumerate(fields):
                c[f - fields[0], i, :, sl] = q_row(f, i, sl) * (1.0 / 3.0) + (2.0 / 3.0) * new[k]


def regroup(lane, n_tiles, fields, s3_ref, c, store):
    rows = s3_ref.shape[1] + 2 * HALO
    block = lane // EDGE
    keep = {bit: (block & bit) == 0 for bit in (1, 2, 4)}

    def final_row(f, r, col):
        if r < HALO:
            return c[f - fields[0], r, :, col]
        if r >= rows - HALO:
            return c[f - fields[0], r - rows + 2 * HALO, :, col]
        return s3_ref[f, r - HALO, :, col]

    @pl.loop(0, n_tiles)
    def _(t):
        col = pl.ds(pl.multiple_of(t * LANES, LANES), LANES)
        for f in fields:
            for half in range(rows // 8):
                v = [final_row(f, half * 8 + r, col) for r in range(8)]
                for bit in (4, 2, 1):
                    for i in range(8):
                        if i & bit:
                            continue
                        lo, hi = v[i], v[i | bit]
                        v[i] = jnp.where(keep[bit], lo, pltpu.roll(hi, bit * EDGE, 1))
                        v[i | bit] = jnp.where(keep[bit], pltpu.roll(lo, LANES - bit * EDGE, 1), hi)
                for d in range(8):
                    store(t, d, (f - fields[0]) * 2 + half, v[d].astype(bf16))


def outer_height_kernel(
    n_rows,
    row_ref,
    near_ref,
    far_ref,
    from_near_ref,
    from_far_ref,
    s1e_ref,
    s2e_ref,
    s3_ref,
    h_ref,
    b,
    q,
    a,
    c,
):
    n_tiles = s3_ref.shape[3] // LANES
    lane = lax.broadcasted_iota(jnp.int32, (8, LANES), 1)

    def place(top_ref, first_ref, last_ref, bottom_ref):
        q[:, 0:3] = top_ref[...]
        q[:, 3:6] = first_ref[...]
        q[:, 6:9] = last_ref[...]
        q[:, 9:12] = bottom_ref[...]
        b[:, 10:13] = first_ref[...]
        b[:, 13:16] = last_ref[...]

    @pl.when(row_ref[0] % 2 == 0)
    def _():
        place(from_far_ref, far_ref, near_ref, from_near_ref)

    @pl.when(row_ref[0] % 2 == 1)
    def _():
        place(from_near_ref, near_ref, far_ref, from_far_ref)

    a[:, 3:7] = s1e_ref[...]
    b[:, 3:7] = s2e_ref[...]

    def q_row(k):
        return lambda f, sl: q[f, k, :, sl]

    def clear(ref, top_at, bottom_at):
        @pl.when(row_ref[0] == 0)
        def _():
            ref[:, top_at] = jnp.zeros_like(ref[:, top_at])

        @pl.when(row_ref[0] == n_rows - 1)
        def _():
            ref[:, bottom_at] = jnp.zeros_like(ref[:, bottom_at])

    every = (0, 1, 2)
    edge_section(
        q, a, lane, n_tiles, every, lambda i, low: (i + 1 + 4 * low, i + 4 * low, None), lambda s, q0: s
    )
    clear(a, 1, 8)
    edge_section(
        a,
        b,
        lane,
        n_tiles,
        every,
        lambda i, low: (i + 1 + 2 * low, i + 4 * low, q_row(i + 2 + 2 * low)),
        lambda s, q0: 0.75 * q0() + 0.25 * s,
    )
    clear(b, 0, 9)
    final_section(lane, n_tiles, (0,), lambda f, i, sl: b[f, 10 + i, :, sl], b, c)

    def store(t, d, k, cells):
        h_ref[t * 8 + d, k] = cells

    regroup(lane, n_tiles, (0,), s3_ref, c, store)


def outer_wind_kernel(at_ref, b_ref, s3_ref, uv_ref, c):
    n_tiles = s3_ref.shape[3] // LANES
    lane = lax.broadcasted_iota(jnp.int32, (8, LANES), 1)
    final_section(lane, n_tiles, (1, 2), lambda f, i, sl: b_ref[f, 10 + i, :, sl], b_ref, c)
    ring = at_ref[0] % RING

    def store(t, d, k, cells):
        uv_ref[(d % RING) ^ ring, t * (8 // RING) + d // RING, k] = cells

    regroup(lane, n_tiles, (1, 2), s3_ref, c, store)


def outer_heights(row, near, far, from_near, from_far, s1e, s2e, s3):
    fields, _, members, columns = s3.shape
    n_dest = columns // EDGE

    def scratch(f, n):
        return pltpu.VMEM((f, n, members, columns), f32)

    return pl.pallas_call(
        functools.partial(outer_height_kernel, lax.axis_size("lat")),
        out_shape=(
            jax.ShapeDtypeStruct((n_dest, 2, members, LANES), bf16),
            jax.ShapeDtypeStruct((fields, 16, members, columns), f32),
        ),
        in_specs=[smem_spec()] + [vmem_spec()] * 7,
        out_specs=(vmem_spec(), vmem_spec()),
        scratch_shapes=[
            scratch(fields, 12),
            scratch(fields, 10),
            scratch(1, 6),
        ],
        compiler_params=pltpu.CompilerParams(vmem_limit_bytes=16 << 20),
        cost_estimate=pl.CostEstimate(flops=2 * 10**8, bytes_accessed=4 * 10**6, transcendentals=0),
        name="outer_heights",
    )(row, near, far, from_near, from_far, s1e, s2e, s3)


def outer_winds(at, b, s3):
    _, _, members, columns = s3.shape
    return pl.pallas_call(
        outer_wind_kernel,
        out_shape=jax.ShapeDtypeStruct((RING, columns // EDGE // RING, 4, members, LANES), bf16),
        in_specs=[smem_spec()] + [vmem_spec()] * 2,
        out_specs=vmem_spec(),
        scratch_shapes=[pltpu.VMEM((2, 2 * HALO, members, columns), f32)],
        compiler_params=pltpu.CompilerParams(vmem_limit_bytes=12 << 20),
        cost_estimate=pl.CostEstimate(flops=10**8, bytes_accessed=4 * 10**6, transcendentals=0),
        name="outer_winds",
    )(at, b, s3)


def ring_kernel(at_ref, *refs):
    out_ref = refs[-1]
    ring = at_ref[0] % RING
    for s, ref in enumerate(refs[:-1]):
        out_ref[:, ring ^ s] = ref[...]


def ring_line(at, pieces):
    first, *rest = pieces[0].shape
    return pl.pallas_call(
        ring_kernel,
        out_shape=jax.ShapeDtypeStruct((first, RING, *rest), bf16),
        in_specs=[smem_spec()] + [vmem_spec()] * RING,
        out_specs=vmem_spec(),
        compiler_params=pltpu.CompilerParams(vmem_limit_bytes=4 << 20),
        name="ring",
    )(at, *pieces)


def split3(row):
    high = row.astype(bf16)
    rest = row - high.astype(f32)
    mid = rest.astype(bf16)
    low = (rest - mid.astype(f32)).astype(bf16)
    zero = jnp.zeros((5, row.shape[1]), f32)
    return jnp.concatenate([high.astype(f32), mid.astype(f32), low.astype(f32), zero], axis=0).astype(bf16)


def centred(slab):
    value = slab.astype(f32).reshape(-1, LANES)
    mean = jnp.sum(value, axis=0, keepdims=True) * (1.0 / value.shape[0])
    return mean, (value - mean).astype(bf16)


def prepare_kernel(at_ref, count_ref, cell_ref, value_ref, rinv_ref, pick_ref, weight_ref):
    at = at_ref[0]
    cells, slots = pick_ref.shape
    place = lax.broadcasted_iota(jnp.int32, (cells, slots), 0)
    pick_ref[...] = jnp.where(place == cell_ref[pl.ds(at, 1), :], 1.0, 0.0).astype(bf16)
    slot = lax.broadcasted_iota(jnp.int32, (1, slots), 1)
    weight = jnp.where(slot < count_ref[0, at], jnp.sqrt(rinv_ref[pl.ds(at, 1), :]), 0.0)
    weight_ref[0:1] = weight
    weight_ref[1:2] = value_ref[pl.ds(at, 1), :]


def prepare(at, count, cell, value, rinv):
    slots = cell.shape[1]
    return pl.pallas_call(
        prepare_kernel,
        out_shape=(
            jax.ShapeDtypeStruct((EDGE * EDGE, slots), bf16),
            jax.ShapeDtypeStruct((2, slots), f32),
        ),
        in_specs=[smem_spec(), smem_spec()] + [vmem_spec()] * 3,
        out_specs=(vmem_spec(), vmem_spec()),
        compiler_params=pltpu.CompilerParams(vmem_limit_bytes=4 << 20),
        name="prepare",
    )(at, count, cell, value, rinv)


def block_kernel(pick_ref, weight_ref, h_ref, out_ref):
    members = h_ref.shape[0] * h_ref.shape[2]
    slots = pick_ref.shape[1]
    weight = weight_ref[0:1]
    hx = jnp.zeros((members, slots), f32)
    for half in range(2):
        _, deviation = centred(h_ref[:, half])
        pick = pick_ref[half * LANES : (half + 1) * LANES]
        hx = hx + jnp.dot(deviation, pick, preferred_element_type=f32)
    centre = jnp.sum(hx, axis=0, keepdims=True) * (1.0 / members)
    scaled = (weight * (hx - centre) * (1.0 / math.sqrt(members - 1))).astype(bf16)
    misfit = weight * (weight_ref[1:2] - centre)
    summary = lax.dot_general(
        split3(misfit), scaled, (((1,), (1,)), ((), ())), preferred_element_type=f32
    )
    summary = jnp.sum(summary, axis=0, keepdims=True)
    out_ref[:members] = scaled
    pieces = [summary[:, i * LANES : (i + 1) * LANES] for i in range(members // LANES)]
    pieces.append(jnp.zeros((8 - len(pieces), LANES), f32))
    out_ref[members:] = jnp.concatenate(pieces, axis=0).astype(bf16)


def make_block(pick, weight, h):
    members = h.shape[0] * h.shape[2]
    return pl.pallas_call(
        block_kernel,
        out_shape=jax.ShapeDtypeStruct((members + 8, pick.shape[1]), bf16),
        in_specs=[vmem_spec()] * 3,
        out_specs=vmem_spec(),
        compiler_params=pltpu.CompilerParams(vmem_limit_bytes=16 << 20),
        name="block",
    )(pick, weight, h)


def stack_kernel(west_ref, own_ref, east_ref, out_ref):
    for k, ref in enumerate((west_ref, own_ref, east_ref)):
        out_ref[k] = ref[...]


def stack_line(west, own, east):
    return pl.pallas_call(
        stack_kernel,
        out_shape=jax.ShapeDtypeStruct((3,) + own.shape, own.dtype),
        in_specs=[vmem_spec()] * 3,
        out_specs=vmem_spec(),
        compiler_params=pltpu.CompilerParams(vmem_limit_bytes=4 << 20),
        name="line",
    )(west, own, east)


def transform_kernel(own_ref, west_ref, east_ref, north_ref, south_ref, out_ref):
    n = out_ref.shape[0]

    def gram_of(refs):
        y = jnp.concatenate([r[:n] for r in refs], axis=1)
        return lax.dot_general(y, y, (((1,), (1,)), ((), ())), preferred_element_type=f32)

    def drive_of(refs):
        total = refs[0][n:].astype(f32)
        for r in refs[1:]:
            total = total + r[n:].astype(f32)
        return total

    centre = [own_ref]
    edges = [west_ref, east_ref, north_ref.at[1], south_ref.at[1]]
    corners = [north_ref.at[0], north_ref.at[2], south_ref.at[0], south_ref.at[2]]
    drive = drive_of(centre) + EDGE_WEIGHT * drive_of(edges) + CORNER_WEIGHT * drive_of(corners)
    drive = jnp.concatenate([drive[i : i + 1] for i in range(n // LANES)], axis=1)
    gram = gram_of(centre) + EDGE_WEIGHT * gram_of(edges) + CORNER_WEIGHT * gram_of(corners)
    diagonal = lax.broadcasted_iota(jnp.int32, (n, n), 0) == lax.broadcasted_iota(jnp.int32, (n, n), 1)
    half_scale = 1.0 / NEWTON_SCALE
    root = (gram * half_scale + jnp.where(diagonal, half_scale, 0.0)).astype(bf16)
    shifted = jnp.where(diagonal, 1.5, 0.0)
    product = root.astype(f32)
    inverse = None
    for sweep in range(NS_ITERS):
        if sweep > 0:
            product = jnp.dot(root, inverse, preferred_element_type=f32)
        correction = (shifted - 0.5 * product).astype(bf16)
        if sweep + 1 < NS_ITERS:
            root = jnp.dot(correction, root, preferred_element_type=f32).astype(bf16)
        if sweep == 0:
            inverse = correction
        else:
            inverse = jnp.dot(inverse, correction, preferred_element_type=f32).astype(bf16)

    def apply(row):
        return jnp.sum(jnp.dot(split3(row), inverse, preferred_element_type=f32), axis=0, keepdims=True)

    weights = apply(apply(drive)) * (1.0 / NEWTON_SCALE / math.sqrt(n - 1))
    out_ref[...] = (weights + inverse.astype(f32) * (1.0 / math.sqrt(NEWTON_SCALE))).astype(bf16)


def make_transform(own, west, east, north, south):
    n = own.shape[0] - 8
    return pl.pallas_call(
        transform_kernel,
        out_shape=jax.ShapeDtypeStruct((n, n), bf16),
        in_specs=[vmem_spec()] * 5,
        out_specs=vmem_spec(),
        name="transform",
        compiler_params=pltpu.CompilerParams(vmem_limit_bytes=24 << 20),
    )(own, west, east, north, south)


def analysed_field(transform_ref, slab, f, out_ref, buffer, sems, at):
    for half in range(2):
        mean, deviation = centred(slab(half))
        buffer[f, :, half * LANES : (half + 1) * LANES] = mean + jnp.dot(
            transform_ref[...], deviation, preferred_element_type=f32
        )
    copy = pltpu.make_async_copy(buffer.at[f], out_ref.at[at], sems.at[f])
    copy.start()
    return copy


def height_kernel(transform_ref, h_ref, out_ref, buffer, sems):
    analysed_field(transform_ref, lambda half: h_ref[:, half], 0, out_ref, buffer, sems, 0).wait()


def wind_kernel(transform_ref, uv_ref, _, out_ref, buffer, sems):
    copies = [
        analysed_field(
            transform_ref, lambda half, f=f: uv_ref[:, 2 * f + half], f, out_ref, buffer, sems, f + 1
        )
        for f in range(2)
    ]
    for c in copies:
        c.wait()


def analyse(transform, h, uv_of):
    n = transform.shape[0]
    cells = EDGE * EDGE
    shape = jax.ShapeDtypeStruct((3, n, cells), f32)
    hbm = pl.BlockSpec(memory_space=pltpu.HBM)
    params = pltpu.CompilerParams(vmem_limit_bytes=8 << 20)
    part = pl.pallas_call(
        height_kernel,
        out_shape=shape,
        in_specs=[vmem_spec()] * 2,
        out_specs=hbm,
        scratch_shapes=[pltpu.VMEM((1, n, cells), f32), pltpu.SemaphoreType.DMA((1,))],
        compiler_params=params,
        cost_estimate=pl.CostEstimate(flops=2 * n * n * cells, bytes_accessed=10**6, transcendentals=0),
        name="heights",
    )(transform, h)
    return pl.pallas_call(
        wind_kernel,
        out_shape=shape,
        in_specs=[vmem_spec()] * 2 + [hbm],
        out_specs=hbm,
        scratch_shapes=[pltpu.VMEM((2, n, cells), f32), pltpu.SemaphoreType.DMA((2,))],
        input_output_aliases={2: 0},
        compiler_params=params,
        name="wind_analysis",
    )(transform, uv_of, part)


def swap(part, axis, start):
    size = lax.axis_size(axis)
    pairs = [(i, i + 1) for i in range(start, size - 1, 2)]
    return lax.ppermute(part, axis, pairs + [(j, i) for i, j in pairs])


def per_device(ensemble_height_winds, obs_count, obs_cell, obs_value, obs_rinv):
    at = lax.axis_index("mem").astype(jnp.int32).reshape(1)
    row = lax.axis_index("lat").astype(jnp.int32).reshape(1)

    q = ensemble_height_winds.transpose(1, 2, 0, 3)
    near, far = edge_rows(row, q)
    from_near = swap(near, "lat", 0)
    from_far = swap(far, "lat", 1)
    s3, s1e, s2e = inner_forecast(q)
    h, edge = outer_heights(row, near, far, from_near, from_far, s1e, s2e, s3)
    uv = outer_winds(at, edge, s3)

    size = lax.axis_size("mem")

    def around(part, shift):
        return lax.ppermute(
            part, "mem", [(i, i ^ shift) for i in range(size)]
        )

    def exchange(part):
        return lax.all_to_all(part, "mem", split_axis=0, concat_axis=0, tiled=True)

    h = exchange(h)
    pick, weight = prepare(at, obs_count, obs_cell[0], obs_value[0], obs_rinv[0])
    own = make_block(pick, weight, h)
    pieces = [uv[0]] + [around(uv[s], s) for s in range(1, RING)]
    uv = ring_line(at, pieces)
    uv = lax.all_to_all(
        uv,
        "mem",
        split_axis=0,
        concat_axis=0,
        axis_index_groups=[list(range(i, size, RING)) for i in range(RING)],
        tiled=True,
    ).reshape(h.shape[0], 4, *h.shape[2:])
    west = swap(own, "mem", 1)
    east = swap(own, "mem", 0)
    line = stack_line(west, own, east)
    north = swap(line, "lat", 1)
    south = swap(line, "lat", 0)
    transform = make_transform(own, west, east, north, south)
    analysed = analyse(transform, h, uv)
    return analysed.transpose(1, 0, 2)[None, None]


def solution(mesh):
    in_specs = (
        P("mem", None, "lat", None),
        P("lat", None),
        P("lat", None, None),
        P("lat", None, None),
        P("lat", None, None),
    )
    out_specs = P("lat", "mem", None, None, None)
    return jax.shard_map(
        per_device, mesh=mesh, in_specs=in_specs, out_specs=out_specs, check_vma=False
    )
```

```python
import functools
import math


import jax
import jax.numpy as jnp
from jax import lax
from jax.experimental import pallas as pl
from jax.experimental.pallas import tpu as pltpu
from jax.sharding import PartitionSpec as P

EDGE = 16
NS_ITERS = 5
EDGE_WEIGHT = 0.6
CORNER_WEIGHT = 0.35
NEWTON_SCALE = 16.0
HALO = 3
RING = 4
LANES = 128

bf16 = jnp.bfloat16
f32 = jnp.float32


def vmem_spec():
    return pl.BlockSpec(memory_space=pltpu.VMEM)


def smem_spec():
    return pl.BlockSpec(memory_space=pltpu.SMEM)


def tile_shifts(load, n, lane):
    tiles, ahead, behind = {}, {}, {}

    def get(t):
        if t not in tiles:
            tiles[t] = load(t)
            ahead[t] = pltpu.roll(tiles[t], LANES - 1, 1)
            behind[t] = pltpu.roll(tiles[t], 1, 1)

    def at(t):
        get(t)
        if t + 1 < n:
            get(t + 1)
        edge = ahead[t + 1] if t + 1 < n else jnp.zeros_like(tiles[t])
        plus = jnp.where(lane == LANES - 1, edge, ahead[t])
        edge = behind[t - 1] if t > 0 else jnp.zeros_like(tiles[t])
        minus = jnp.where(lane == 0, edge, behind[t])
        return tiles[t], plus - minus

    return at


def advance(src, i, lane, n_tiles, fields=(0, 1, 2)):
    def load(f, k):
        return lambda t: src[f, k, :, t * LANES : (t + 1) * LANES]

    h_at = tile_shifts(load(0, i), n_tiles, lane)
    u_at = tile_shifts(load(1, i), n_tiles, lane)
    v_at = tile_shifts(load(2, i), n_tiles, lane)
    flux_at = tile_shifts(
        lambda t: (1.0 + load(0, i)(t)) * load(1, i)(t), n_tiles, lane
    )
    for t in range(n_tiles):
        hu, hd = load(0, i + 1)(t), load(0, i - 1)(t)
        vu, vd = load(2, i + 1)(t), load(2, i - 1)(t)
        new = []
        if 0 in fields:
            _, df = flux_at(t)
            dyf = (1.0 + hu) * vu - (1.0 + hd) * vd
            new.append(load(0, i)(t) - 0.25 * (df + dyf))
        if 1 in fields:
            _, dh = h_at(t)
            u, du = u_at(t)
            v, dv = v_at(t)
            dyu = load(1, i + 1)(t) - load(1, i - 1)(t)
            qu, qv = 0.25 * u, 0.25 * v
            new.append(u - (qu * du + qv * (dyu - 0.5) + 0.25 * dh))
            new.append(v - (qu * (dv + 0.5) + qv * (vu - vd) + 0.25 * (hu - hd)))
        yield t, new


def edge_kernel(row_ref, q_ref, near_ref, far_ref):
    rows = q_ref.shape[1]

    def place(first_ref, last_ref):
        first_ref[...] = q_ref[:, :HALO]
        last_ref[...] = q_ref[:, rows - HALO :]

    @pl.when(row_ref[0] % 2 == 0)
    def _():
        place(far_ref, near_ref)

    @pl.when(row_ref[0] % 2 == 1)
    def _():
        place(near_ref, far_ref)


def edge_rows(row, q):
    fields, _, members, columns = q.shape
    part = jax.ShapeDtypeStruct((fields, HALO, members, columns), f32)
    return pl.pallas_call(
        edge_kernel,
        out_shape=(part, part),
        in_specs=[smem_spec(), vmem_spec()],
        out_specs=(vmem_spec(), vmem_spec()),
        compiler_params=pltpu.CompilerParams(vmem_limit_bytes=4 << 20),
        name="edges",
    )(row, q)


def inner_kernel(q, s3_ref, s1e_ref, s2e_ref, a, b):
    rows = q.shape[1]
    n_tiles = q.shape[3] // LANES
    lane = lax.broadcasted_iota(jnp.int32, (8, LANES), 1)

    def section(src, dst, lo, hi, off, combine):
        @pl.loop(lo, hi, unroll=2)
        def _(i):
            for t, new in advance(src, i, lane, n_tiles):
                sl = slice(t * LANES, (t + 1) * LANES)
                for f in range(3):
                    dst[f, i - off, :, sl] = combine(new[f], lambda: q[f, i, :, sl])

    section(q, a, 1, rows - 1, 0, lambda s, q0: s)
    section(a, b, 2, rows - 2, 0, lambda s, q0: 0.75 * q0() + 0.25 * s)
    section(b, s3_ref, 3, rows - 3, 3, lambda s, q0: q0() * (1.0 / 3.0) + (2.0 / 3.0) * s)
    s1e_ref[:, :2] = a[:, 1:3]
    s1e_ref[:, 2:] = a[:, rows - 3 : rows - 1]
    s2e_ref[:, :2] = b[:, 2:4]
    s2e_ref[:, 2:] = b[:, rows - 4 : rows - 2]


def inner_forecast(q):
    fields, rows, members, columns = q.shape

    def part(n):
        return jax.ShapeDtypeStruct((fields, n, members, columns), f32)

    return pl.pallas_call(
        inner_kernel,
        out_shape=(part(rows - 2 * HALO), part(4), part(4)),
        in_specs=[vmem_spec()],
        out_specs=(vmem_spec(),) * 3,
        scratch_shapes=[pltpu.VMEM((fields, rows, members, columns), f32)] * 2,
        compiler_params=pltpu.CompilerParams(vmem_limit_bytes=12 << 20),
        cost_estimate=pl.CostEstimate(flops=4 * 10**8, bytes_accessed=4 * 10**6, transcendentals=0),
        name="inner",
    )(q)


def edge_section(src, dst, lane, n_tiles, fields, places, combine):
    @pl.loop(0, 2 * HALO, unroll=2 * HALO)
    def _(i):
        at, to, q_row = places(i, (i >= HALO).astype(jnp.int32))
        for t, new in advance(src, at, lane, n_tiles, fields):
            sl = slice(t * LANES, (t + 1) * LANES)
            for k, f in enumerate(fields):
                dst[f - fields[0], to, :, sl] = combine(new[k], lambda: q_row(f, sl))


def final_section(lane, n_tiles, fields, q_row, b, c):
    for i in range(2 * HALO):
        at = i + 1 if i < HALO else i + 3
        for t, new in advance(b, at, lane, n_tiles, fields):
            sl = slice(t * LANES, (t + 1) * LANES)
            for k, f in enumerate(fields):
                c[f - fields[0], i, :, sl] = q_row(f, i, sl) * (1.0 / 3.0) + (2.0 / 3.0) * new[k]


def regroup(lane, n_tiles, fields, s3_ref, c, store):
    rows = s3_ref.shape[1] + 2 * HALO
    block = lane // EDGE
    keep = {bit: (block & bit) == 0 for bit in (1, 2, 4)}

    def final_row(f, r, col):
        if r < HALO:
            return c[f - fields[0], r, :, col]
        if r >= rows - HALO:
            return c[f - fields[0], r - rows + 2 * HALO, :, col]
        return s3_ref[f, r - HALO, :, col]

    @pl.loop(0, n_tiles)
    def _(t):
        col = pl.ds(pl.multiple_of(t * LANES, LANES), LANES)
        for f in fields:
            for half in range(rows // 8):
                v = [final_row(f, half * 8 + r, col) for r in range(8)]
                for bit in (4, 2, 1):
                    for i in range(8):
                        if i & bit:
                            continue
                        lo, hi = v[i], v[i | bit]
                        v[i] = jnp.where(keep[bit], lo, pltpu.roll(hi, bit * EDGE, 1))
                        v[i | bit] = jnp.where(keep[bit], pltpu.roll(lo, LANES - bit * EDGE, 1), hi)
                for d in range(8):
                    store(t, d, (f - fields[0]) * 2 + half, v[d].astype(bf16))


def outer_height_kernel(
    n_rows,
    row_ref,
    near_ref,
    far_ref,
    from_near_ref,
    from_far_ref,
    s1e_ref,
    s2e_ref,
    s3_ref,
    h_ref,
    b,
    q,
    a,
    c,
):
    n_tiles = s3_ref.shape[3] // LANES
    lane = lax.broadcasted_iota(jnp.int32, (8, LANES), 1)

    def place(top_ref, first_ref, last_ref, bottom_ref):
        q[:, 0:3] = top_ref[...]
        q[:, 3:6] = first_ref[...]
        q[:, 6:9] = last_ref[...]
        q[:, 9:12] = bottom_ref[...]
        b[:, 10:13] = first_ref[...]
        b[:, 13:16] = last_ref[...]

    @pl.when(row_ref[0] % 2 == 0)
    def _():
        place(from_far_ref, far_ref, near_ref, from_near_ref)

    @pl.when(row_ref[0] % 2 == 1)
    def _():
        place(from_near_ref, near_ref, far_ref, from_far_ref)

    a[:, 3:7] = s1e_ref[...]
    b[:, 3:7] = s2e_ref[...]

    def q_row(k):
        return lambda f, sl: q[f, k, :, sl]

    def clear(ref, top_at, bottom_at):
        @pl.when(row_ref[0] == 0)
        def _():
            ref[:, top_at] = jnp.zeros_like(ref[:, top_at])

        @pl.when(row_ref[0] == n_rows - 1)
        def _():
            ref[:, bottom_at] = jnp.zeros_like(ref[:, bottom_at])

    every = (0, 1, 2)
    edge_section(
        q, a, lane, n_tiles, every, lambda i, low: (i + 1 + 4 * low, i + 4 * low, None), lambda s, q0: s
    )
    clear(a, 1, 8)
    edge_section(
        a,
        b,
        lane,
        n_tiles,
        every,
        lambda i, low: (i + 1 + 2 * low, i + 4 * low, q_row(i + 2 + 2 * low)),
        lambda s, q0: 0.75 * q0() + 0.25 * s,
    )
    clear(b, 0, 9)
    final_section(lane, n_tiles, (0,), lambda f, i, sl: b[f, 10 + i, :, sl], b, c)

    def store(t, d, k, cells):
        h_ref[t * 8 + d, k] = cells

    regroup(lane, n_tiles, (0,), s3_ref, c, store)


def outer_wind_kernel(at_ref, b_ref, s3_ref, uv_ref, c):
    n_tiles = s3_ref.shape[3] // LANES
    lane = lax.broadcasted_iota(jnp.int32, (8, LANES), 1)
    final_section(lane, n_tiles, (1, 2), lambda f, i, sl: b_ref[f, 10 + i, :, sl], b_ref, c)
    ring = at_ref[0] % RING

    def store(t, d, k, cells):
        uv_ref[(d % RING) ^ ring, t * (8 // RING) + d // RING, k] = cells

    regroup(lane, n_tiles, (1, 2), s3_ref, c, store)


def outer_heights(row, near, far, from_near, from_far, s1e, s2e, s3):
    fields, _, members, columns = s3.shape
    n_dest = columns // EDGE

    def scratch(f, n):
        return pltpu.VMEM((f, n, members, columns), f32)

    return pl.pallas_call(
        functools.partial(outer_height_kernel, lax.axis_size("lat")),
        out_shape=(
            jax.ShapeDtypeStruct((n_dest, 2, members, LANES), bf16),
            jax.ShapeDtypeStruct((fields, 16, members, columns), f32),
        ),
        in_specs=[smem_spec()] + [vmem_spec()] * 7,
        out_specs=(vmem_spec(), vmem_spec()),
        scratch_shapes=[
            scratch(fields, 12),
            scratch(fields, 10),
            scratch(1, 6),
        ],
        compiler_params=pltpu.CompilerParams(vmem_limit_bytes=16 << 20),
        cost_estimate=pl.CostEstimate(flops=2 * 10**8, bytes_accessed=4 * 10**6, transcendentals=0),
        name="outer_heights",
    )(row, near, far, from_near, from_far, s1e, s2e, s3)


def outer_winds(at, b, s3):
    _, _, members, columns = s3.shape
    return pl.pallas_call(
        outer_wind_kernel,
        out_shape=jax.ShapeDtypeStruct((RING, columns // EDGE // RING, 4, members, LANES), bf16),
        in_specs=[smem_spec()] + [vmem_spec()] * 2,
        out_specs=vmem_spec(),
        scratch_shapes=[pltpu.VMEM((2, 2 * HALO, members, columns), f32)],
        compiler_params=pltpu.CompilerParams(vmem_limit_bytes=12 << 20),
        cost_estimate=pl.CostEstimate(flops=10**8, bytes_accessed=4 * 10**6, transcendentals=0),
        name="outer_winds",
    )(at, b, s3)


def ring_kernel(at_ref, *refs):
    out_ref = refs[-1]
    ring = at_ref[0] % RING
    for s, ref in enumerate(refs[:-1]):
        out_ref[:, ring ^ s] = ref[...]


def ring_line(at, pieces):
    first, *rest = pieces[0].shape
    return pl.pallas_call(
        ring_kernel,
        out_shape=jax.ShapeDtypeStruct((first, RING, *rest), bf16),
        in_specs=[smem_spec()] + [vmem_spec()] * RING,
        out_specs=vmem_spec(),
        compiler_params=pltpu.CompilerParams(vmem_limit_bytes=4 << 20),
        name="ring",
    )(at, *pieces)


def split3(row):
    high = row.astype(bf16)
    rest = row - high.astype(f32)
    mid = rest.astype(bf16)
    low = (rest - mid.astype(f32)).astype(bf16)
    zero = jnp.zeros((5, row.shape[1]), f32)
    return jnp.concatenate([high.astype(f32), mid.astype(f32), low.astype(f32), zero], axis=0).astype(bf16)


def centred(slab):
    value = slab.astype(f32).reshape(-1, LANES)
    mean = jnp.sum(value, axis=0, keepdims=True) * (1.0 / value.shape[0])
    return mean, (value - mean).astype(bf16)


def prepare_kernel(at_ref, count_ref, cell_ref, value_ref, rinv_ref, pick_ref, weight_ref):
    at = at_ref[0]
    cells, slots = pick_ref.shape
    place = lax.broadcasted_iota(jnp.int32, (cells, slots), 0)
    pick_ref[...] = jnp.where(place == cell_ref[pl.ds(at, 1), :], 1.0, 0.0).astype(bf16)
    slot = lax.broadcasted_iota(jnp.int32, (1, slots), 1)
    weight = jnp.where(slot < count_ref[0, at], jnp.sqrt(rinv_ref[pl.ds(at, 1), :]), 0.0)
    weight_ref[0:1] = weight
    weight_ref[1:2] = value_ref[pl.ds(at, 1), :]


def prepare(at, count, cell, value, rinv):
    slots = cell.shape[1]
    return pl.pallas_call(
        prepare_kernel,
        out_shape=(
            jax.ShapeDtypeStruct((EDGE * EDGE, slots), bf16),
            jax.ShapeDtypeStruct((2, slots), f32),
        ),
        in_specs=[smem_spec(), smem_spec()] + [vmem_spec()] * 3,
        out_specs=(vmem_spec(), vmem_spec()),
        compiler_params=pltpu.CompilerParams(vmem_limit_bytes=4 << 20),
        name="prepare",
    )(at, count, cell, value, rinv)


def block_kernel(pick_ref, weight_ref, h_ref, out_ref):
    members = h_ref.shape[0] * h_ref.shape[2]
    slots = pick_ref.shape[1]
    weight = weight_ref[0:1]
    hx = jnp.zeros((members, slots), f32)
    for half in range(2):
        _, deviation = centred(h_ref[:, half])
        pick = pick_ref[half * LANES : (half + 1) * LANES]
        hx = hx + jnp.dot(deviation, pick, preferred_element_type=f32)
    centre = jnp.sum(hx, axis=0, keepdims=True) * (1.0 / members)
    scaled = (weight * (hx - centre) * (1.0 / math.sqrt(members - 1))).astype(bf16)
    misfit = weight * (weight_ref[1:2] - centre)
    summary = lax.dot_general(
        split3(misfit), scaled, (((1,), (1,)), ((), ())), preferred_element_type=f32
    )
    summary = jnp.sum(summary, axis=0, keepdims=True)
    out_ref[:members] = scaled
    pieces = [summary[:, i * LANES : (i + 1) * LANES] for i in range(members // LANES)]
    pieces.append(jnp.zeros((8 - len(pieces), LANES), f32))
    out_ref[members:] = jnp.concatenate(pieces, axis=0).astype(bf16)


def make_block(pick, weight, h):
    members = h.shape[0] * h.shape[2]
    return pl.pallas_call(
        block_kernel,
        out_shape=jax.ShapeDtypeStruct((members + 8, pick.shape[1]), bf16),
        in_specs=[vmem_spec()] * 3,
        out_specs=vmem_spec(),
        compiler_params=pltpu.CompilerParams(vmem_limit_bytes=16 << 20),
        name="block",
    )(pick, weight, h)


def stack_kernel(west_ref, own_ref, east_ref, out_ref):
    for k, ref in enumerate((west_ref, own_ref, east_ref)):
        out_ref[k] = ref[...]


def stack_line(west, own, east):
    return pl.pallas_call(
        stack_kernel,
        out_shape=jax.ShapeDtypeStruct((3,) + own.shape, own.dtype),
        in_specs=[vmem_spec()] * 3,
        out_specs=vmem_spec(),
        compiler_params=pltpu.CompilerParams(vmem_limit_bytes=4 << 20),
        name="line",
    )(west, own, east)


def transform_kernel(own_ref, west_ref, east_ref, north_ref, south_ref, out_ref):
    n = out_ref.shape[0]

    def gram_of(refs):
        y = jnp.concatenate([r[:n] for r in refs], axis=1)
        return lax.dot_general(y, y, (((1,), (1,)), ((), ())), preferred_element_type=f32)

    def drive_of(refs):
        total = refs[0][n:].astype(f32)
        for r in refs[1:]:
            total = total + r[n:].astype(f32)
        return total

    centre = [own_ref]
    edges = [west_ref, east_ref, north_ref.at[1], south_ref.at[1]]
    corners = [north_ref.at[0], north_ref.at[2], south_ref.at[0], south_ref.at[2]]
    drive = drive_of(centre) + EDGE_WEIGHT * drive_of(edges) + CORNER_WEIGHT * drive_of(corners)
    drive = jnp.concatenate([drive[i : i + 1] for i in range(n // LANES)], axis=1)
    gram = gram_of(centre) + EDGE_WEIGHT * gram_of(edges) + CORNER_WEIGHT * gram_of(corners)
    diagonal = lax.broadcasted_iota(jnp.int32, (n, n), 0) == lax.broadcasted_iota(jnp.int32, (n, n), 1)
    half_scale = 1.0 / NEWTON_SCALE
    root = (gram * half_scale + jnp.where(diagonal, half_scale, 0.0)).astype(bf16)
    shifted = jnp.where(diagonal, 1.5, 0.0)
    product = root.astype(f32)
    inverse = None
    for sweep in range(NS_ITERS):
        if sweep > 0:
            product = jnp.dot(root, inverse, preferred_element_type=f32)
        correction = (shifted - 0.5 * product).astype(bf16)
        if sweep + 1 < NS_ITERS:
            root = jnp.dot(correction, root, preferred_element_type=f32).astype(bf16)
        if sweep == 0:
            inverse = correction
        else:
            inverse = jnp.dot(inverse, correction, preferred_element_type=f32).astype(bf16)

    def apply(row):
        return jnp.sum(jnp.dot(split3(row), inverse, preferred_element_type=f32), axis=0, keepdims=True)

    weights = apply(apply(drive)) * (1.0 / NEWTON_SCALE / math.sqrt(n - 1))
    out_ref[...] = (weights + inverse.astype(f32) * (1.0 / math.sqrt(NEWTON_SCALE))).astype(bf16)


def make_transform(own, west, east, north, south):
    n = own.shape[0] - 8
    return pl.pallas_call(
        transform_kernel,
        out_shape=jax.ShapeDtypeStruct((n, n), bf16),
        in_specs=[vmem_spec()] * 5,
        out_specs=vmem_spec(),
        name="transform",
        compiler_params=pltpu.CompilerParams(vmem_limit_bytes=24 << 20),
    )(own, west, east, north, south)


def analysed_field(transform_ref, slab, f, out_ref, buffer, sems, at):
    halves = [centred(slab(half)) for half in range(2)]
    mean, deviation = (jnp.concatenate(part, axis=1) for part in zip(*halves))
    buffer[f] = mean + jnp.dot(transform_ref[...], deviation, preferred_element_type=f32)
    copy = pltpu.make_async_copy(buffer.at[f], out_ref.at[at], sems.at[f])
    copy.start()
    return copy


def height_kernel(transform_ref, h_ref, out_ref, buffer, sems):
    analysed_field(transform_ref, lambda half: h_ref[:, half], 0, out_ref, buffer, sems, 0).wait()


def wind_kernel(transform_ref, uv_ref, _, out_ref, buffer, sems):
    copies = [
        analysed_field(
            transform_ref, lambda half, f=f: uv_ref[:, 2 * f + half], f, out_ref, buffer, sems, f + 1
        )
        for f in range(2)
    ]
    for c in copies:
        c.wait()


def analyse(transform, h, uv_of):
    n = transform.shape[0]
    cells = EDGE * EDGE
    shape = jax.ShapeDtypeStruct((3, n, cells), f32)
    hbm = pl.BlockSpec(memory_space=pltpu.HBM)
    params = pltpu.CompilerParams(vmem_limit_bytes=8 << 20)
    part = pl.pallas_call(
        height_kernel,
        out_shape=shape,
        in_specs=[vmem_spec()] * 2,
        out_specs=hbm,
        scratch_shapes=[pltpu.VMEM((1, n, cells), f32), pltpu.SemaphoreType.DMA((1,))],
        compiler_params=params,
        cost_estimate=pl.CostEstimate(flops=2 * n * n * cells, bytes_accessed=10**6, transcendentals=0),
        name="heights",
    )(transform, h)
    return pl.pallas_call(
        wind_kernel,
        out_shape=shape,
        in_specs=[vmem_spec()] * 2 + [hbm],
        out_specs=hbm,
        scratch_shapes=[pltpu.VMEM((2, n, cells), f32), pltpu.SemaphoreType.DMA((2,))],
        input_output_aliases={2: 0},
        compiler_params=params,
        name="wind_analysis",
    )(transform, uv_of, part)


def swap(part, axis, start):
    size = lax.axis_size(axis)
    pairs = [(i, i + 1) for i in range(start, size - 1, 2)]
    return lax.ppermute(part, axis, pairs + [(j, i) for i, j in pairs])


def per_device(ensemble_height_winds, obs_count, obs_cell, obs_value, obs_rinv):
    at = lax.axis_index("mem").astype(jnp.int32).reshape(1)
    row = lax.axis_index("lat").astype(jnp.int32).reshape(1)

    q = ensemble_height_winds.transpose(1, 2, 0, 3)
    near, far = edge_rows(row, q)
    from_near = swap(near, "lat", 0)
    from_far = swap(far, "lat", 1)
    s3, s1e, s2e = inner_forecast(q)
    h, edge = outer_heights(row, near, far, from_near, from_far, s1e, s2e, s3)
    uv = outer_winds(at, edge, s3)

    size = lax.axis_size("mem")

    def around(part, shift):
        return lax.ppermute(
            part, "mem", [(i, i ^ shift) for i in range(size)]
        )

    def exchange(part):
        return lax.all_to_all(part, "mem", split_axis=0, concat_axis=0, tiled=True)

    h = exchange(h)
    pick, weight = prepare(at, obs_count, obs_cell[0], obs_value[0], obs_rinv[0])
    own = make_block(pick, weight, h)
    pieces = [uv[0]] + [around(uv[s], s) for s in range(1, RING)]
    uv = ring_line(at, pieces)
    uv = lax.all_to_all(
        uv,
        "mem",
        split_axis=0,
        concat_axis=0,
        axis_index_groups=[list(range(i, size, RING)) for i in range(RING)],
        tiled=True,
    ).reshape(h.shape[0], 4, *h.shape[2:])
    west = swap(own, "mem", 1)
    east = swap(own, "mem", 0)
    line = stack_line(west, own, east)
    north = swap(line, "lat", 1)
    south = swap(line, "lat", 0)
    transform = make_transform(own, west, east, north, south)
    analysed = analyse(transform, h, uv)
    return analysed.transpose(1, 0, 2)[None, None]


def solution(mesh):
    in_specs = (
        P("mem", None, "lat", None),
        P("lat", None),
        P("lat", None, None),
        P("lat", None, None),
        P("lat", None, None),
    )
    out_specs = P("lat", "mem", None, None, None)
    return jax.shard_map(
        per_device, mesh=mesh, in_specs=in_specs, out_specs=out_specs, check_vma=False
    )
```
